768 devices in a mesh: pipe: 64 (over y, z_hi, core), expert: 12 (over x, z_lo).
Axes of the slice: x: 4, y: 8, z: 12 (z_hi: 4, z_lo: 3; z = z_hi * 3 + z_lo), core: 2. Of those that a mesh axis runs over, the one named last changes fastest.
Arguments:
- flowing: bfloat16 [2, 1152, 14336], P(None, 'expert', 'pipe'), may hold values from -6 to 6
- norm_gain: float32 [14336], P('pipe'), may hold values from 0.5 to 1.5
- gate_up: bfloat16 [12, 64, 896, 1024], P('expert', 'pipe'), may hold values from -0.0625 to 0.0625
- down_proj: bfloat16 [12, 64, 896, 512], P('expert', 'pipe'), may hold values from -0.125 to 0.125
- down_step: bfloat16 [12, 64, 896, 512], P('expert', 'pipe'), may hold values from -0.0625 to 0.0625
- step_rate: float32 [12, 2], P('expert'), may hold values from 0.5 to 2
- routes: int32 [2, 2, 2, 1152, 2], P(None, None, None, 'expert'), may hold values from 0 to 11, all different within a row; in each aligned block of 96 rows (0 to 95, 96 to 191, ..., all dimensions but the last counted through in order) at most 18 rows name the same one
- scores: float32 [2, 2, 2, 1152, 2], P(None, None, None, 'expert'), may hold values from 0.05 to 1
Outputs:
- flowing_out: bfloat16 [2, 1152, 14336], P(None, 'expert', 'pipe')
The draws below stay inside these ranges and needn't reach their ends.
Inputs may be any that keep to these rules, and one draw needn't show every extreme that they name: `routes`: each token names 2 different experts. In each aligned block of 96 rows (the tokens of one expert rank for one step, section and direction) no expert is named by more than 18 rows.
All inputs are finite; a program needn't handle non-finite values.
Results may differ from the reference program's by a relative error of at most 0.02.
Values may be sent and summed in bfloat16 or wider, within the bound.
No kernel may reach another device: no remote copies, remote signals or barrier semaphores. Data moves between devices by JAX's collectives and lax.ppermute only.
A program may use at most 32 MiB of HBM per device.

```python
import math
import jax
import jax.numpy as jnp
import numpy as np
from jax import lax

D = 7168
FF = 2048
SECTIONS = 2
TICKS = 2
TOPK = 2
SR = 96
EXPERTS = 12
ROWS_ALL = 1152
CAP = 18
HSHARDS = 32
HG = 4
WG = 8


def level_of(stream_key, dims, shards, smallest, top_value):
    level, own = 1.0, jax.random.fold_in(stream_key, 6)
    for axis_at, blocks in shards:
        heights = jnp.exp(jax.random.uniform(jax.random.fold_in(own, axis_at), (blocks,), jnp.float32, smallest / len(shards), top_value / len(shards)))
        level = level * jnp.repeat(heights, dims[axis_at] // blocks).reshape([-1 if axis == axis_at else 1 for axis in range(len(dims))])
    return level


def assign_block(key, own, number, rows, count, top, most, slope):
    order = jax.random.permutation(key, count)
    packed, usual = load_shares(count, rows * top, most, slope, True), load_shares(count, rows * top, most, slope, False)
    places = jnp.arange(count)

    def named(sizes, offset_by):
        used = int((sizes > 0).sum())
        fixed = max(1, used // 4)
        moved = fixed + (places - fixed + offset_by * (used - fixed)) % max(1, count - fixed)
        return jnp.zeros((count,), jnp.int32).at[order[jnp.where(places < fixed, places, moved)]].set(jnp.asarray(sizes, jnp.int32))

    sizes = jnp.where(number % 4 == 0, named(packed, number // 4), named(usual, number - number // 4 - 1))
    mixed = jax.random.permutation(jax.random.fold_in(own, 3), count)
    source_of, taker = mixed[0:count // 2 * 2:2], mixed[1:count // 2 * 2:2]
    slack = jnp.minimum(sizes[source_of] - 1, most - sizes[taker]) // 2
    slack = jnp.where((source_of == order[0]) | (taker == order[0]) | (sizes[taker] == 0), 0, jnp.maximum(slack, 0))
    moved = jax.random.randint(jax.random.fold_in(own, 4), (count // 2,), 0, 1 << 20) % (slack + 1)
    sizes = sizes.at[source_of].add(-moved).at[taker].add(moved)
    items = jnp.searchsorted(jnp.cumsum(sizes), jnp.arange(rows * top), side="right").astype(jnp.int32)
    grid = items.reshape(top, rows).T
    grid = grid[jax.random.permutation(jax.random.fold_in(own, 1), rows)]
    offset_by = jax.random.randint(jax.random.fold_in(own, 2), (rows, 1), 0, top)
    return jnp.take_along_axis(grid, (jnp.arange(top)[None, :] + offset_by) % top, axis=1)


def load_shares(number_of, total, reach, skew, full):
    weights = [(1 << 20) // math.isqrt(grade ** skew) + 1 for grade in range(1, number_of + 1)]
    largest = reach if full else min(reach, max(-(-total // number_of), total * weights[0] // sum(weights)))
    least = 1 if total - largest >= number_of - 1 else 0
    given, spare = [largest] + [least] * (number_of - 1), total - largest - least * (number_of - 1)
    while spare > 0:
        candidates = [i for i in range(1, number_of) if given[i] < largest] or [i for i in range(1, number_of) if given[i] < reach]
        pool, left = sum([weights[i] for i in candidates]), spare
        for i in candidates:
            more = min(reach - given[i], max(1, left * weights[i] // pool), spare)
            given[i] = given[i] + more
            spare = spare - more
    return np.array(given)


def scatter_about(stream_key, shape, spread, bound, pieces=(), kind=jnp.bfloat16):
    gain = level_of(stream_key, shape, pieces, -0.22, 0.18) if pieces else 1.0
    values = jax.random.normal(stream_key, shape, jnp.float32) * spread * gain
    return jnp.minimum(jnp.maximum(values, -bound), bound).astype(kind)


def setup_inputs(seed: int = 0) -> dict:
    streams_of = jax.random.split(jax.random.key(seed), 9)
    flowing = scatter_about(streams_of[0], (2, ROWS_ALL, SECTIONS * D), 1.0, 6.0, ((1, 12), (2, 64)))
    norm_gain = jnp.clip(1.0 + 0.1 * jax.random.normal(streams_of[1], (SECTIONS * D,), jnp.float32), 0.5, 1.5)
    gate_up = scatter_about(streams_of[2], (EXPERTS, SECTIONS * HSHARDS, D // WG, 2 * FF // HG), D ** -0.5, 0.0625, ((0, 12), (1, 64)))
    down_proj = scatter_about(streams_of[3], (EXPERTS, SECTIONS * HSHARDS, D // WG, FF // HG), FF ** -0.5, 0.125, ((0, 12), (1, 64)))
    down_step = scatter_about(streams_of[4], (EXPERTS, SECTIONS * HSHARDS, D // WG, FF // HG), (4 * FF) ** -0.5, 0.0625, ((0, 12), (1, 64)))
    step_rate = jnp.clip(jnp.exp(math.log(2.0) - 1.3862944 * jax.random.uniform(streams_of[5], (EXPERTS, SECTIONS), jnp.float32) ** level_of(streams_of[5], (EXPERTS, SECTIONS), ((0, 12),), -0.2, 0.2)), 0.5, 2.0)
    routes_keys = jax.random.split(jax.random.fold_in(streams_of[6], 1), TICKS * SECTIONS * 2 * ROWS_ALL // SR)
    routes_turns = jax.random.permutation(jax.random.fold_in(streams_of[6], 3), TICKS * SECTIONS * 2 * ROWS_ALL // SR)
    routes = jax.vmap(lambda own, number: assign_block(jax.random.fold_in(streams_of[6], 2), own, number, SR, EXPERTS, TOPK, CAP, 2))(routes_keys, routes_turns).reshape((TICKS, SECTIONS, 2, ROWS_ALL, TOPK))
    scores = jnp.clip(jnp.exp(math.log(1.0) - 2.9957323 * jax.random.uniform(streams_of[7], (TICKS, SECTIONS, 2, ROWS_ALL, TOPK), jnp.float32) ** level_of(streams_of[7], (TICKS, SECTIONS, 2, ROWS_ALL, TOPK), ((3, 12),), -0.2, 0.2)), 0.05, 1.0)
    return {"flowing": flowing, "norm_gain": norm_gain, "gate_up": gate_up, "down_proj": down_proj, "down_step": down_step, "step_rate": step_rate, "routes": routes, "scores": scores}


EPS = 1e-06
ROUTE_SCALE = 2.5

def section_layer(section_rows, section_gain, gate_up, down_proj, down_step, step_rate, section_index, route_ids, route_scores):
    values = section_rows.astype(jnp.float32)
    squares = lax.optimization_barrier(jnp.sum(values * values, axis=1))
    scaling = lax.rsqrt(squares / D + EPS)
    prepared = (values * section_gain).astype(jnp.bfloat16)
    expert_count = gate_up.shape[0]
    slot_count = EXPERTS * CAP
    flat_route = route_ids.reshape(-1).astype(jnp.int32)
    one_hot = (flat_route[:, None] == jnp.arange(expert_count, dtype=jnp.int32)[None, :]).astype(jnp.int32)
    position = lax.optimization_barrier(jnp.sum((jnp.cumsum(one_hot, axis=0) - one_hot) * one_hot, axis=1)).astype(jnp.int32)
    token_of = (jnp.arange(flat_route.shape[0], dtype=jnp.int32) // TOPK).astype(jnp.int32)
    buffer = jnp.zeros((expert_count, slot_count, D), jnp.bfloat16).at[flat_route, position].set(prepared[token_of])
    slot_scale = jnp.zeros((expert_count, slot_count), jnp.float32).at[flat_route, position].set(scaling[token_of])
    block_start = jnp.asarray(section_index * HSHARDS, jnp.int32)
    zero_index = jnp.asarray(0, jnp.int32)

    def run_expert(expert_index):
        rows_in = buffer[expert_index]
        row_scale = slot_scale[expert_index]
        blocks_in = lax.dynamic_slice(gate_up, (expert_index, block_start, zero_index, zero_index), (1, HSHARDS, D // WG, 2 * FF // HG))[0]
        weights_in = blocks_in.reshape(WG, HG, D // WG, 2, FF // HG).transpose(0, 2, 3, 1, 4).reshape(D, 2 * FF)
        blocks_out = lax.dynamic_slice(down_proj, (expert_index, block_start, zero_index, zero_index), (1, HSHARDS, D // WG, FF // HG))[0]
        blocks_step = lax.dynamic_slice(down_step, (expert_index, block_start, zero_index, zero_index), (1, HSHARDS, D // WG, FF // HG))[0]
        weights_out = blocks_out.reshape(WG, HG, D // WG, FF // HG).transpose(0, 2, 1, 3).reshape(D, FF).astype(jnp.float32)
        update = blocks_step.reshape(WG, HG, D // WG, FF // HG).transpose(0, 2, 1, 3).reshape(D, FF).astype(jnp.float32)
        extrapolated = (weights_out + step_rate[expert_index, section_index] * update).astype(jnp.bfloat16)
        projected = jnp.dot(rows_in, weights_in, preferred_element_type=jnp.float32) * row_scale[:, None]
        activated = (jax.nn.silu(projected[:, :FF]) * projected[:, FF:]).astype(jnp.bfloat16)
        return jnp.dot(activated, extrapolated.T, preferred_element_type=jnp.float32).astype(jnp.bfloat16)
    results = lax.map(run_expert, jnp.arange(expert_count, dtype=jnp.int32))
    picked = results[flat_route, position].astype(jnp.float32).reshape(section_rows.shape[0], TOPK, D)
    mixing = ROUTE_SCALE * route_scores / lax.optimization_barrier(jnp.sum(route_scores, axis=1, keepdims=True))
    return (values + lax.optimization_barrier(jnp.sum(mixing[:, :, None] * picked, axis=1))).astype(jnp.bfloat16)

def reference(flowing, norm_gain, gate_up, down_proj, down_step, step_rate, routes, scores):
    row_total = flowing.shape[1]
    carried = flowing.reshape(2, row_total, SECTIONS, D)
    for tick_index in range(TICKS):
        section_blocks = []
        for section_index in range(SECTIONS):
            section_gain = norm_gain[section_index * D:(section_index + 1) * D]
            both_dirs = [section_layer(carried[direction, :, section_index], section_gain, gate_up, down_proj, down_step, step_rate, section_index, routes[tick_index, section_index, direction], scores[tick_index, section_index, direction]) for direction in range(2)]
            section_blocks.append(jnp.stack(both_dirs))
        layer_out = jnp.stack(section_blocks, axis=2)
        if tick_index + 1 < TICKS:
            layer_out = jnp.stack([jnp.roll(layer_out[0], 1, axis=1), jnp.roll(layer_out[1], -1, axis=1)])
        carried = layer_out
    return carried.reshape(2, row_total, SECTIONS * D)
```

```python
import jax
import jax.numpy as jnp
from jax import lax
from jax.experimental import pallas as pl
from jax.experimental.pallas import tpu as pltpu
from jax.sharding import PartitionSpec as P

D = 7168
FF = 2048
EPS = 1e-06
ROUTE_SCALE = 2.5
LANES = 256
SQ_TILE = 16
DOT_ROWS = (((1,), (1,)), ((), ()))


def exchange(x, bit):
    size = lax.axis_size("pipe")
    return lax.ppermute(x, "pipe", [(i, i ^ (1 << bit)) for i in range(size)])


def other_section(x):
    size = lax.axis_size("pipe")
    return lax.ppermute(x, "pipe", [(i, (i + size // 2) % size) for i in range(size)])


def weight_kernel(where, gate_up, down, step, rate, w_in, w_out):
    h, y = where[0], where[1]
    cols = gate_up.shape[0] // 4
    w_in[...] = jnp.zeros_like(w_in)
    w_out[...] = jnp.zeros_like(w_out)
    for block in range(4):
        rows = pl.ds(pl.multiple_of((h ^ ((block & 1) * 2 + (block >> 1))) * cols, 32), cols)
        for place, rel in enumerate((0, 2, 1, 3)):
            at = pl.multiple_of((y ^ rel) * 128, 128)
            to = slice(block * LANES, block * LANES + cols)
            w_in[to, place * 256 : place * 256 + 128] = gate_up[rows, pl.ds(at, 128)]
            w_in[to, place * 256 + 128 : place * 256 + 256] = gate_up[
                rows, pl.ds(pl.multiple_of(512 + at, 128), 128)
            ]
            w_out[to, place * 128 : place * 128 + 128] = (
                down[rows, pl.ds(at, 128)].astype(jnp.float32)
                + rate[0] * step[rows, pl.ds(at, 128)].astype(jnp.float32)
            ).astype(jnp.bfloat16)


def arrange_weights(where, rate, gate_up, down, step):
    vmem = pl.BlockSpec(memory_space=pltpu.VMEM)
    smem = pl.BlockSpec(memory_space=pltpu.SMEM)
    return pl.pallas_call(
        weight_kernel,
        out_shape=(
            jax.ShapeDtypeStruct((4 * LANES, gate_up.shape[1]), jnp.bfloat16),
            jax.ShapeDtypeStruct((4 * LANES, down.shape[1]), jnp.bfloat16),
        ),
        in_specs=[smem, vmem, vmem, vmem, smem],
        out_specs=(vmem, vmem),
        cost_estimate=pl.CostEstimate(flops=2000000, bytes_accessed=8000000, transcendentals=0),
    )(where, gate_up, down, step, rate)


def routing(route_ids, route_scores, expert_count, capacity):
    lead, rows, picks = route_ids.shape
    flat = route_ids.reshape(lead, rows * picks)
    one_hot = (flat[:, :, None] == jnp.arange(expert_count, dtype=jnp.int32)).astype(jnp.int32)
    position = jnp.sum((jnp.cumsum(one_hot, axis=1) - one_hot) * one_hot, axis=2)
    slot = (flat * capacity + position).reshape(lead, rows, picks)
    slot_ids = jnp.arange(expert_count * capacity, dtype=jnp.int32)
    chosen = (slot[..., None] == slot_ids).astype(jnp.float32)
    mixing = ROUTE_SCALE * route_scores / jnp.sum(route_scores, axis=2, keepdims=True)
    mix = jnp.sum(mixing[..., None] * chosen, axis=2)
    return jnp.sum(chosen, axis=2).astype(jnp.bfloat16), mix


def layer(state, spread, mix, gain, w_in, w_out, expert_count, capacity):
    lead, rows, cols = state.shape
    values = state.astype(jnp.float32)
    squares = jnp.sum(values * values, axis=2, keepdims=True)
    high = squares.astype(jnp.bfloat16)
    low = (squares - high.astype(jnp.float32)).astype(jnp.bfloat16)
    tail = jnp.zeros((lead, rows, LANES - cols - 2), jnp.bfloat16)
    prepared = jnp.concatenate([(values * gain).astype(jnp.bfloat16), high, low, tail], axis=2)
    both = jnp.concatenate([prepared, exchange(prepared, 1)], axis=2)
    buffer = jnp.einsum("nrs,nrc->nsc", spread, both, preferred_element_type=jnp.float32)
    buffer = buffer.astype(jnp.bfloat16).reshape(lead, expert_count, capacity, 2 * LANES)
    arrived = lax.all_to_all(
        buffer.transpose(1, 0, 2, 3), "expert", split_axis=0, concat_axis=0, tiled=True
    )
    slots = expert_count * lead * capacity
    arrived = arrived.reshape(slots, 2 * LANES)
    inputs = jnp.concatenate([arrived, exchange(arrived, 0)], axis=1)
    lane = jnp.arange(4 * LANES) % LANES
    marks = ((lane == cols) | (lane == cols + 1)).astype(jnp.bfloat16)
    marks = jnp.broadcast_to(marks[None], (SQ_TILE, 4 * LANES))
    half = LANES
    sums = [
        lax.dot_general(marks, part, DOT_ROWS, preferred_element_type=jnp.float32)
        for part in (inputs[:half], inputs[half:])
    ]
    sums[1] = jnp.pad(sums[1], ((0, 0), (0, 2 * half - slots)))
    index = jnp.arange(SQ_TILE)[:, None]
    sums = jnp.where(index == 0, sums[0], jnp.where(index == 1, sums[1], 0.0))
    partial = jnp.dot(inputs, w_in, preferred_element_type=jnp.float32)
    width = partial.shape[1]
    for bit in (3, 4):
        width //= 2
        message = jnp.concatenate(
            [
                partial[:, width:].astype(jnp.bfloat16),
                jnp.pad(sums, ((0, 0), (0, width - half))).astype(jnp.bfloat16),
            ],
            axis=0,
        )
        got = exchange(message, bit).astype(jnp.float32)
        partial = partial[:, :width] + got[:slots]
        sums = sums + got[slots:, :half]
    message = jnp.concatenate([partial, sums], axis=0).astype(jnp.bfloat16)
    got = exchange(message, 2).astype(jnp.float32)
    partial = partial + got[:slots]
    sums = sums + got[slots:]
    scaling = lax.rsqrt(jnp.concatenate([sums[0], sums[1, : slots - half]]) / D + EPS)[:, None]
    projected = partial * scaling
    activated = (jax.nn.silu(projected[:, :128]) * projected[:, 128:]).astype(jnp.bfloat16)
    for bit in (4, 3):
        activated = jnp.concatenate([activated, exchange(activated, bit)], axis=1)
    partial = lax.dot_general(activated, w_out, DOT_ROWS, preferred_element_type=jnp.float32)
    got = exchange(partial[:, 2 * LANES :].astype(jnp.bfloat16), 0)
    expert_out = (partial[:, : 2 * LANES] + got.astype(jnp.float32)).astype(jnp.bfloat16)
    expert_out = expert_out.reshape(expert_count, lead, capacity, 2 * LANES)
    returned = lax.all_to_all(expert_out, "expert", split_axis=0, concat_axis=0, tiled=True)
    returned = returned.transpose(1, 0, 2, 3).reshape(lead, expert_count * capacity, 2 * LANES)
    mix_high = mix.astype(jnp.bfloat16)
    mix_low = (mix - mix_high.astype(jnp.float32)).astype(jnp.bfloat16)
    mixed = sum(
        jnp.einsum("nrs,nsc->nrc", part, returned, preferred_element_type=jnp.float32)
        for part in (mix_high, mix_low)
    )
    got = exchange(mixed[:, :, LANES:].astype(jnp.bfloat16), 1)
    mixed = mixed[:, :, :cols] + got[:, :, :cols].astype(jnp.float32)
    return (values + mixed).astype(jnp.bfloat16)


def body(flowing, norm_gain, gate_up, down_proj, down_step, step_rate, routes, scores):
    shards = lax.axis_size("pipe") // step_rate.shape[1]
    my_index = lax.axis_index("pipe")
    section = my_index // shards
    expert_count = lax.axis_size("expert")
    capacity = flowing.shape[1] * routes.shape[-1] // expert_count + 2
    where = jnp.stack([my_index & 3, (my_index >> 3) & 3]).astype(jnp.int32)
    rate = lax.dynamic_slice_in_dim(step_rate[0], section, 1, 0)
    w_in, w_out = arrange_weights(where, rate, gate_up[0, 0], down_proj[0, 0], down_step[0, 0])
    route_here = lax.dynamic_index_in_dim(routes, section, 1, keepdims=False)
    score_here = lax.dynamic_index_in_dim(scores, section, 1, keepdims=False)
    ticks = routes.shape[0]
    state = flowing
    for tick in range(ticks):
        spread, mix = routing(route_here[tick], score_here[tick], expert_count, capacity)
        state = layer(state, spread, mix, norm_gain, w_in, w_out, expert_count, capacity)
        if tick + 1 < ticks:
            state = other_section(state)
    return state


def solution(mesh):
    placed = (
        P(None, "expert", "pipe"),
        P("pipe"),
        P("expert", "pipe", None, None),
        P("expert", "pipe", None, None),
        P("expert", "pipe", None, None),
        P("expert", None),
        P(None, None, None, "expert", None),
        P(None, None, None, "expert", None),
    )
    return jax.shard_map(
        body, mesh=mesh, in_specs=placed, out_specs=P(None, "expert", "pipe"), check_vma=False
    )
```

```python
import jax
import jax.numpy as jnp
from jax import lax
from jax.experimental import pallas as pl
from jax.experimental.pallas import tpu as pltpu
from jax.sharding import PartitionSpec as P

D = 7168
FF = 2048
EPS = 1e-06
ROUTE_SCALE = 2.5
LANES = 256
SQ_TILE = 8
LEAD = 2
TIE = True
DOT_ROWS = (((1,), (1,)), ((), ()))


def exchange(x, bit):
    size = lax.axis_size("pipe")
    return lax.ppermute(x, "pipe", [(i, i ^ (1 << bit)) for i in range(size)])


def other_section(x):
    size = lax.axis_size("pipe")
    return lax.ppermute(x, "pipe", [(i, (i + size // 2) % size) for i in range(size)])


def weight_kernel(where, gate_up, down, step, rate, w_in, w_out):
    h, y = where[0], where[1]
    cols = gate_up.shape[0] // 4
    w_in[...] = jnp.zeros_like(w_in)
    w_out[...] = jnp.zeros_like(w_out)
    for block in range(4):
        rows = pl.ds(pl.multiple_of((h ^ ((block & 1) * 2 + (block >> 1))) * cols, 32), cols)
        for place, rel in enumerate((0, 2, 1, 3)):
            at = pl.multiple_of((y ^ rel) * 128, 128)
            to = slice(block * LANES, block * LANES + cols)
            w_in[to, place * 256 : place * 256 + 128] = gate_up[rows, pl.ds(at, 128)]
            w_in[to, place * 256 + 128 : place * 256 + 256] = gate_up[
                rows, pl.ds(pl.multiple_of(512 + at, 128), 128)
            ]
            w_out[to, place * 128 : place * 128 + 128] = (
                down[rows, pl.ds(at, 128)].astype(jnp.float32)
                + rate[0] * step[rows, pl.ds(at, 128)].astype(jnp.float32)
            ).astype(jnp.bfloat16)


def arrange_weights(where, rate, gate_up, down, step):
    vmem = pl.BlockSpec(memory_space=pltpu.VMEM)
    smem = pl.BlockSpec(memory_space=pltpu.SMEM)
    return pl.pallas_call(
        weight_kernel,
        out_shape=(
            jax.ShapeDtypeStruct((4 * LANES, gate_up.shape[1]), jnp.bfloat16),
            jax.ShapeDtypeStruct((4 * LANES, down.shape[1]), jnp.bfloat16),
        ),
        in_specs=[smem, vmem, vmem, vmem, smem],
        out_specs=(vmem, vmem),
        cost_estimate=pl.CostEstimate(flops=2000000, bytes_accessed=8000000, transcendentals=0),
    )(where, gate_up, down, step, rate)


def routing(route_ids, route_scores, expert_count, capacity):
    lead, rows, picks = route_ids.shape
    flat = route_ids.reshape(lead, rows * picks)
    one_hot = (flat[:, :, None] == jnp.arange(expert_count, dtype=jnp.int32)).astype(jnp.int32)
    position = jnp.sum((jnp.cumsum(one_hot, axis=1) - one_hot) * one_hot, axis=2)
    slot = (flat * capacity + position).reshape(lead, rows, picks)
    slot_ids = jnp.arange(expert_count * capacity, dtype=jnp.int32)
    chosen = (slot[..., None] == slot_ids).astype(jnp.float32)
    mixing = ROUTE_SCALE * route_scores / jnp.sum(route_scores, axis=2, keepdims=True)
    mix = jnp.sum(mixing[..., None] * chosen, axis=2)
    return jnp.sum(chosen, axis=2).astype(jnp.bfloat16), mix


def tied(x, *others):
    return lax.optimization_barrier((x, *others))[0]


def layer(state, spread, mix, gain, w_in, w_out, expert_count, capacity):
    rows, cols = state.shape
    slots = expert_count * capacity
    values = state.astype(jnp.float32)
    squares = jnp.sum(values * values, axis=1, keepdims=True)
    high = squares.astype(jnp.bfloat16)
    low = (squares - high.astype(jnp.float32)).astype(jnp.bfloat16)
    tail = jnp.zeros((rows, LANES - cols - 2), jnp.bfloat16)
    prepared = jnp.concatenate([(values * gain).astype(jnp.bfloat16), high, low, tail], axis=1)
    prepared = yield "gather", prepared
    both = jnp.concatenate([prepared, exchange(prepared, 1)], axis=1)
    buffer = lax.dot_general(
        spread, both, (((0,), (0,)), ((), ())), preferred_element_type=jnp.float32
    ).astype(jnp.bfloat16)
    buffer = yield "dispatch", buffer.reshape(expert_count, capacity, 2 * LANES)
    arrived = lax.all_to_all(buffer, "expert", split_axis=0, concat_axis=0, tiled=True)
    arrived = arrived.reshape(slots, 2 * LANES)
    arrived = yield "cores", arrived
    inputs = jnp.concatenate([arrived, exchange(arrived, 0)], axis=1)
    lane = jnp.arange(4 * LANES) % LANES
    marks = ((lane == cols) | (lane == cols + 1)).astype(jnp.bfloat16)
    marks = jnp.broadcast_to(marks[None], (SQ_TILE, 4 * LANES))
    sums = lax.dot_general(marks, inputs, DOT_ROWS, preferred_element_type=jnp.float32)
    partial = jnp.dot(inputs, w_in, preferred_element_type=jnp.float32)
    width = partial.shape[1]
    for name, bit in (("near", 3), ("far", 4)):
        width //= 2
        message = jnp.concatenate(
            [
                partial[:, width:].astype(jnp.bfloat16),
                jnp.pad(sums, ((0, 0), (0, width - slots))).astype(jnp.bfloat16),
            ],
            axis=0,
        )
        message = yield name, message
        got = exchange(message, bit).astype(jnp.float32)
        partial = partial[:, :width] + got[:slots]
        sums = sums + got[slots:, :slots]
    message = jnp.concatenate([partial, jnp.pad(sums, ((0, 0), (0, width - slots)))], axis=0)
    message = yield "across", message.astype(jnp.bfloat16)
    got = exchange(message, 2).astype(jnp.float32)
    partial = partial + got[:slots]
    sums = sums[0] + got[slots, :slots]
    scaling = lax.rsqrt(sums / D + EPS)[:, None]
    projected = partial * scaling
    activated = (jax.nn.silu(projected[:, :128]) * projected[:, 128:]).astype(jnp.bfloat16)
    for name, bit in (("hidden_far", 4), ("hidden_near", 3)):
        activated = yield name, activated
        activated = jnp.concatenate([activated, exchange(activated, bit)], axis=1)
    partial = lax.dot_general(activated, w_out, DOT_ROWS, preferred_element_type=jnp.float32)
    message = yield "out_cores", partial[:, 2 * LANES :].astype(jnp.bfloat16)
    got = exchange(message, 0)
    expert_out = (partial[:, : 2 * LANES] + got.astype(jnp.float32)).astype(jnp.bfloat16)
    expert_out = yield "back", expert_out.reshape(expert_count, capacity, 2 * LANES)
    returned = lax.all_to_all(expert_out, "expert", split_axis=0, concat_axis=0, tiled=True)
    returned = returned.reshape(slots, 2 * LANES)
    mix_high = mix.astype(jnp.bfloat16)
    mix_low = (mix - mix_high.astype(jnp.float32)).astype(jnp.bfloat16)
    mixed = sum(
        jnp.dot(part, returned, preferred_element_type=jnp.float32) for part in (mix_high, mix_low)
    )
    message = yield "out_gather", mixed[:, LANES:].astype(jnp.bfloat16)
    got = exchange(message, 1)
    mixed = mixed[:, :cols] + got[:, :cols].astype(jnp.float32)
    return (values + mixed).astype(jnp.bfloat16)


def window(state, direction, spreads, mixes, *rest):
    ticks = len(spreads)
    for tick in range(ticks):
        state = yield from layer(state, spreads[tick][direction], mixes[tick][direction], *rest)
        if tick + 1 < ticks:
            state = yield "relay", state
            state = other_section(state)
    return state


def interleaved(first, second, lead, tie):
    outs, sent, turn, done = [None, None], [None, None], 0, 0
    streams = [first, second]
    alive = [True, True]
    step = [0, 0]

    def advance(which):
        try:
            if step[which] == 0:
                name, message = next(streams[which])
            else:
                name, message = streams[which].send(sent[which])
            other = sent[1 - which]
            if tie and other is not None:
                message = tied(message, other)
            sent[which] = message
            step[which] += 1
        except StopIteration as end:
            outs[which] = end.value
            alive[which] = False

    while alive[0] or alive[1]:
        if alive[0]:
            advance(0)
        if alive[1] and (step[0] - step[1] >= lead or not alive[0]):
            advance(1)
    return outs


def body(flowing, norm_gain, gate_up, down_proj, down_step, step_rate, routes, scores):
    shards = lax.axis_size("pipe") // step_rate.shape[1]
    my_index = lax.axis_index("pipe")
    section = my_index // shards
    expert_count = lax.axis_size("expert")
    capacity = flowing.shape[1] * routes.shape[-1] // expert_count + 2
    where = jnp.stack([my_index & 3, (my_index >> 3) & 3]).astype(jnp.int32)
    rate = lax.dynamic_slice_in_dim(step_rate[0], section, 1, 0)
    w_in, w_out = arrange_weights(where, rate, gate_up[0, 0], down_proj[0, 0], down_step[0, 0])
    route_here = lax.dynamic_index_in_dim(routes, section, 1, keepdims=False)
    score_here = lax.dynamic_index_in_dim(scores, section, 1, keepdims=False)
    ticks = routes.shape[0]
    spreads, mixes = [], []
    for tick in range(ticks):
        spread, mix = routing(route_here[tick], score_here[tick], expert_count, capacity)
        spreads.append(spread)
        mixes.append(mix)
    streams = [
        window(flowing[d], d, spreads, mixes, norm_gain, w_in, w_out, expert_count, capacity)
        for d in range(2)
    ]
    return jnp.stack(interleaved(*streams, LEAD, TIE))


def solution(mesh):
    placed = (
        P(None, "expert", "pipe"),
        P("pipe"),
        P("expert", "pipe", None, None),
        P("expert", "pipe", None, None),
        P("expert", "pipe", None, None),
        P("expert", None),
        P(None, None, None, "expert", None),
        P(None, None, None, "expert", None),
    )
    return jax.shard_map(
        body, mesh=mesh, in_specs=placed, out_specs=P(None, "expert", "pipe"), check_vma=False
    )
```

```python
import jax
import jax.numpy as jnp
from jax import lax
from jax.experimental import pallas as pl
from jax.experimental.pallas import tpu as pltpu
from jax.sharding import PartitionSpec as P

D = 7168
FF = 2048
EPS = 1e-06
ROUTE_SCALE = 2.5
LANES = 256
SQ_TILE = 16
DOT_ROWS = (((1,), (1,)), ((), ()))


def exchange(x, bit):
    size = lax.axis_size("pipe")
    return lax.ppermute(x, "pipe", [(i, i ^ (1 << bit)) for i in range(size)])


def along_y(x, apart):
    size = lax.axis_size("pipe")
    return lax.ppermute(x, "pipe", [(i, i ^ (apart << 3)) for i in range(size)])


def other_section(x):
    size = lax.axis_size("pipe")
    return lax.ppermute(x, "pipe", [(i, (i + size // 2) % size) for i in range(size)])


def weight_kernel(where, gate_up, down, step, rate, w_in, w_out):
    h, y = where[0], where[1]
    cols = gate_up.shape[0] // 4
    w_in[...] = jnp.zeros_like(w_in)
    w_out[...] = jnp.zeros_like(w_out)
    for block in range(4):
        rows = pl.ds(pl.multiple_of((h ^ ((block & 1) * 2 + (block >> 1))) * cols, 32), cols)
        for place, rel in enumerate(range(4)):
            at = pl.multiple_of((y ^ rel) * 128, 128)
            to = slice(block * LANES, block * LANES + cols)
            w_in[to, place * 256 : place * 256 + 128] = gate_up[rows, pl.ds(at, 128)]
            w_in[to, place * 256 + 128 : place * 256 + 256] = gate_up[
                rows, pl.ds(pl.multiple_of(512 + at, 128), 128)
            ]
            w_out[to, place * 128 : place * 128 + 128] = (
                down[rows, pl.ds(at, 128)].astype(jnp.float32)
                + rate[0] * step[rows, pl.ds(at, 128)].astype(jnp.float32)
            ).astype(jnp.bfloat16)


def arrange_weights(where, rate, gate_up, down, step):
    vmem = pl.BlockSpec(memory_space=pltpu.VMEM)
    smem = pl.BlockSpec(memory_space=pltpu.SMEM)
    return pl.pallas_call(
        weight_kernel,
        out_shape=(
            jax.ShapeDtypeStruct((4 * LANES, gate_up.shape[1]), jnp.bfloat16),
            jax.ShapeDtypeStruct((4 * LANES, down.shape[1]), jnp.bfloat16),
        ),
        in_specs=[smem, vmem, vmem, vmem, smem],
        out_specs=(vmem, vmem),
        cost_estimate=pl.CostEstimate(flops=2000000, bytes_accessed=8000000, transcendentals=0),
    )(where, gate_up, down, step, rate)


def routing(route_ids, route_scores, expert_count, capacity):
    lead, rows, picks = route_ids.shape
    flat = route_ids.reshape(lead, rows * picks)
    one_hot = (flat[:, :, None] == jnp.arange(expert_count, dtype=jnp.int32)).astype(jnp.int32)
    position = jnp.sum((jnp.cumsum(one_hot, axis=1) - one_hot) * one_hot, axis=2)
    slot = (flat * capacity + position).reshape(lead, rows, picks)
    slot_ids = jnp.arange(expert_count * capacity, dtype=jnp.int32)
    chosen = (slot[..., None] == slot_ids).astype(jnp.float32)
    mixing = ROUTE_SCALE * route_scores / jnp.sum(route_scores, axis=2, keepdims=True)
    mix = jnp.sum(mixing[..., None] * chosen, axis=2)
    return jnp.sum(chosen, axis=2).astype(jnp.bfloat16), mix


def layer(state, spread, mix, gain, w_in, w_out, expert_count, capacity):
    lead, rows, cols = state.shape
    values = state.astype(jnp.float32)
    squares = jnp.sum(values * values, axis=2, keepdims=True)
    high = squares.astype(jnp.bfloat16)
    low = (squares - high.astype(jnp.float32)).astype(jnp.bfloat16)
    tail = jnp.zeros((lead, rows, LANES - cols - 2), jnp.bfloat16)
    prepared = jnp.concatenate([(values * gain).astype(jnp.bfloat16), high, low, tail], axis=2)
    got, w_in, w_out = lax.optimization_barrier((exchange(prepared, 1), w_in, w_out))
    both = jnp.concatenate([prepared, got], axis=2)
    buffer = jnp.einsum("nrs,nrc->nsc", spread, both, preferred_element_type=jnp.float32)
    buffer = buffer.astype(jnp.bfloat16).reshape(lead, expert_count, capacity, 2 * LANES)
    arrived = lax.all_to_all(
        buffer.transpose(1, 0, 2, 3), "expert", split_axis=0, concat_axis=0, tiled=True
    )
    slots = expert_count * lead * capacity
    arrived = arrived.reshape(slots, 2 * LANES)
    inputs = jnp.concatenate([arrived, exchange(arrived, 0)], axis=1)
    lane = jnp.arange(4 * LANES) % LANES
    marks = ((lane == cols) | (lane == cols + 1)).astype(jnp.bfloat16)
    marks = jnp.broadcast_to(marks[None], (SQ_TILE, 4 * LANES))
    half = LANES
    sums = [
        lax.dot_general(marks, part, DOT_ROWS, preferred_element_type=jnp.float32)
        for part in (inputs[:half], inputs[half:])
    ]
    sums[1] = jnp.pad(sums[1], ((0, 0), (0, 2 * half - slots)))
    index = jnp.arange(SQ_TILE)[:, None]
    sums = jnp.where(index == 0, sums[0], jnp.where(index == 1, sums[1], 0.0))
    partial = jnp.dot(inputs, w_in, preferred_element_type=jnp.float32)
    got = [
        along_y(
            jnp.concatenate(
                [partial[:, apart * 256 : apart * 256 + 256].astype(jnp.bfloat16), sums.astype(jnp.bfloat16)]
            ),
            apart,
        )
        for apart in (3, 2, 1)
    ]
    got = sum(part.astype(jnp.float32) for part in got)
    partial = partial[:, :256] + got[:slots]
    sums = sums + got[slots:]
    message = jnp.concatenate([partial, sums], axis=0).astype(jnp.bfloat16)
    got = exchange(message, 2).astype(jnp.float32)
    partial = partial + got[:slots]
    sums = sums + got[slots:]
    scaling = lax.rsqrt(jnp.concatenate([sums[0], sums[1, : slots - half]]) / D + EPS)[:, None]
    projected = partial * scaling
    activated = (jax.nn.silu(projected[:, :128]) * projected[:, 128:]).astype(jnp.bfloat16)
    got = [along_y(activated, apart) for apart in (3, 2, 1)]
    activated = jnp.concatenate([activated, *got[::-1]], axis=1)
    partial = lax.dot_general(activated, w_out, DOT_ROWS, preferred_element_type=jnp.float32)
    got = exchange(partial[:, 2 * LANES :].astype(jnp.bfloat16), 0)
    expert_out = (partial[:, : 2 * LANES] + got.astype(jnp.float32)).astype(jnp.bfloat16)
    expert_out = expert_out.reshape(expert_count, lead, capacity, 2 * LANES)
    returned = lax.all_to_all(expert_out, "expert", split_axis=0, concat_axis=0, tiled=True)
    returned = returned.transpose(1, 0, 2, 3).reshape(lead, expert_count * capacity, 2 * LANES)
    mix_high = mix.astype(jnp.bfloat16)
    mix_low = (mix - mix_high.astype(jnp.float32)).astype(jnp.bfloat16)
    mixed = sum(
        jnp.einsum("nrs,nsc->nrc", part, returned, preferred_element_type=jnp.float32)
        for part in (mix_high, mix_low)
    )
    got = exchange(mixed[:, :, LANES:].astype(jnp.bfloat16), 1)
    mixed = mixed[:, :, :cols] + got[:, :, :cols].astype(jnp.float32)
    return (values + mixed).astype(jnp.bfloat16)


def body(flowing, norm_gain, gate_up, down_proj, down_step, step_rate, routes, scores):
    shards = lax.axis_size("pipe") // step_rate.shape[1]
    my_index = lax.axis_index("pipe")
    section = my_index // shards
    expert_count = lax.axis_size("expert")
    capacity = flowing.shape[1] * routes.shape[-1] // expert_count + 2
    where = jnp.stack([my_index & 3, (my_index >> 3) & 3]).astype(jnp.int32)
    rate = lax.dynamic_slice_in_dim(step_rate[0], section, 1, 0)
    w_in, w_out = arrange_weights(where, rate, gate_up[0, 0], down_proj[0, 0], down_step[0, 0])
    route_here = lax.dynamic_index_in_dim(routes, section, 1, keepdims=False)
    score_here = lax.dynamic_index_in_dim(scores, section, 1, keepdims=False)
    ticks = routes.shape[0]
    state = flowing
    for tick in range(ticks):
        spread, mix = routing(route_here[tick], score_here[tick], expert_count, capacity)
        state = layer(state, spread, mix, norm_gain, w_in, w_out, expert_count, capacity)
        if tick + 1 < ticks:
            state = other_section(state)
    return state


def solution(mesh):
    placed = (
        P(None, "expert", "pipe"),
        P("pipe"),
        P("expert", "pipe", None, None),
        P("expert", "pipe", None, None),
        P("expert", "pipe", None, None),
        P("expert", None),
        P(None, None, None, "expert", None),
        P(None, None, None, "expert", None),
    )
    return jax.shard_map(
        body, mesh=mesh, in_specs=placed, out_specs=P(None, "expert", "pipe"), check_vma=False
    )
```

```python
import jax
import jax.numpy as jnp
from jax import lax
from jax.experimental import pallas as pl
from jax.experimental.pallas import tpu as pltpu
from jax.sharding import PartitionSpec as P

D = 7168
FF = 2048
EPS = 1e-06
ROUTE_SCALE = 2.5
LANES = 256
SQ_TILE = 8
DOT_ROWS = (((1,), (1,)), ((), ()))


def exchange(x, bit):
    size = lax.axis_size("pipe")
    return lax.ppermute(x, "pipe", [(i, i ^ (1 << bit)) for i in range(size)])


def along_y(x, apart):
    size = lax.axis_size("pipe")
    return lax.ppermute(x, "pipe", [(i, i ^ (apart << 3)) for i in range(size)])


def other_section(x):
    size = lax.axis_size("pipe")
    return lax.ppermute(x, "pipe", [(i, (i + size // 2) % size) for i in range(size)])


def weight_kernel(where, gate_up, down, step, rate, w_in, w_out):
    h, y = where[0], where[1]
    cols = gate_up.shape[0] // 4
    w_in[...] = jnp.zeros_like(w_in)
    w_out[...] = jnp.zeros_like(w_out)
    for block in range(4):
        rows = pl.ds(pl.multiple_of((h ^ ((block & 1) * 2 + (block >> 1))) * cols, 32), cols)
        for place, rel in enumerate(range(4)):
            at = pl.multiple_of((y ^ rel) * 128, 128)
            to = slice(block * LANES, block * LANES + cols)
            w_in[to, place * 256 : place * 256 + 128] = gate_up[rows, pl.ds(at, 128)]
            w_in[to, place * 256 + 128 : place * 256 + 256] = gate_up[
                rows, pl.ds(pl.multiple_of(512 + at, 128), 128)
            ]
            w_out[to, place * 128 : place * 128 + 128] = (
                down[rows, pl.ds(at, 128)].astype(jnp.float32)
                + rate[0] * step[rows, pl.ds(at, 128)].astype(jnp.float32)
            ).astype(jnp.bfloat16)


def arrange_weights(where, rate, gate_up, down, step):
    vmem = pl.BlockSpec(memory_space=pltpu.VMEM)
    smem = pl.BlockSpec(memory_space=pltpu.SMEM)
    return pl.pallas_call(
        weight_kernel,
        out_shape=(
            jax.ShapeDtypeStruct((4 * LANES, gate_up.shape[1]), jnp.bfloat16),
            jax.ShapeDtypeStruct((4 * LANES, down.shape[1]), jnp.bfloat16),
        ),
        in_specs=[smem, vmem, vmem, vmem, smem],
        out_specs=(vmem, vmem),
        cost_estimate=pl.CostEstimate(flops=2000000, bytes_accessed=8000000, transcendentals=0),
    )(where, gate_up, down, step, rate)


def routing(route_ids, route_scores, expert_count, capacity):
    lead, rows, picks = route_ids.shape
    flat = route_ids.reshape(lead, rows * picks)
    one_hot = (flat[:, :, None] == jnp.arange(expert_count, dtype=jnp.int32)).astype(jnp.int32)
    position = jnp.sum((jnp.cumsum(one_hot, axis=1) - one_hot) * one_hot, axis=2)
    slot = (flat * capacity + position).reshape(lead, rows, picks)
    slot_ids = jnp.arange(expert_count * capacity, dtype=jnp.int32)
    chosen = (slot[..., None] == slot_ids).astype(jnp.float32)
    mixing = ROUTE_SCALE * route_scores / jnp.sum(route_scores, axis=2, keepdims=True)
    mix = jnp.sum(mixing[..., None] * chosen, axis=2)
    return jnp.sum(chosen, axis=2).astype(jnp.bfloat16), mix


def layer(state, spread, mix, gain, w_in, w_out, expert_count, capacity):
    lead, rows, cols = state.shape
    values = state.astype(jnp.float32)
    squares = jnp.sum(values * values, axis=2, keepdims=True)
    high = squares.astype(jnp.bfloat16)
    low = (squares - high.astype(jnp.float32)).astype(jnp.bfloat16)
    tail = jnp.zeros((lead, rows, LANES - cols - 2), jnp.bfloat16)
    prepared = jnp.concatenate([(values * gain).astype(jnp.bfloat16), high, low, tail], axis=2)
    got, w_in, w_out = lax.optimization_barrier((exchange(prepared, 1), w_in, w_out))
    both = jnp.concatenate([prepared, got], axis=2)
    buffer = jnp.einsum("nrs,nrc->nsc", spread, both, preferred_element_type=jnp.float32)
    buffer = buffer.astype(jnp.bfloat16).reshape(lead, expert_count, capacity, 2 * LANES)
    arrived = lax.all_to_all(
        buffer.transpose(1, 0, 2, 3), "expert", split_axis=0, concat_axis=0, tiled=True
    )
    slots = expert_count * lead * capacity
    arrived = arrived.reshape(slots, 2 * LANES)
    inputs = jnp.concatenate([arrived, exchange(arrived, 0)], axis=1)
    lane = jnp.arange(4 * LANES) % LANES
    marks = ((lane == cols) | (lane == cols + 1)).astype(jnp.bfloat16)
    marks = jnp.broadcast_to(marks[None], (SQ_TILE, 4 * LANES))
    half = slots // 2
    parts = [inputs[:half], inputs[half:]]
    blocks = [jnp.dot(part, w_in, preferred_element_type=jnp.float32) for part in parts]
    sums = [
        lax.dot_general(marks, part, DOT_ROWS, preferred_element_type=jnp.float32)
        for part in parts
    ]
    sums = [jnp.pad(row, ((0, 0), (0, LANES - half))) for row in sums]
    summed = []
    for partial, row in zip(blocks, sums):
        packed = [
            jnp.concatenate([partial[:, k * 256 : k * 256 + 256], row]).astype(jnp.bfloat16)
            for k in (3, 2, 1)
        ]
        if summed:
            packed, _ = lax.optimization_barrier((packed, first))
        first = packed
        got = [along_y(message, k) for message, k in zip(packed, (3, 2, 1))]
        got = sum(message.astype(jnp.float32) for message in got)
        summed.append(jnp.concatenate([partial[:, :256], row]) + got)
    crossed = [total + exchange(total.astype(jnp.bfloat16), 2).astype(jnp.float32) for total in summed]
    hidden = []
    for total in crossed:
        scaling = lax.rsqrt(total[half, :half] / D + EPS)[:, None]
        projected = total[:half] * scaling
        hidden.append(
            (jax.nn.silu(projected[:, :128]) * projected[:, 128:]).astype(jnp.bfloat16)
        )
    outs = []
    for piece in hidden:
        got = [along_y(piece, k) for k in (3, 2, 1)]
        piece = jnp.concatenate([piece, *got[::-1]], axis=1)
        outs.append(
            lax.dot_general(piece, w_out, DOT_ROWS, preferred_element_type=jnp.float32)
        )
    partial = jnp.concatenate(outs)
    got = exchange(partial[:, 2 * LANES :].astype(jnp.bfloat16), 0)
    expert_out = (partial[:, : 2 * LANES] + got.astype(jnp.float32)).astype(jnp.bfloat16)
    expert_out = expert_out.reshape(expert_count, lead, capacity, 2 * LANES)
    returned = lax.all_to_all(expert_out, "expert", split_axis=0, concat_axis=0, tiled=True)
    returned = returned.transpose(1, 0, 2, 3).reshape(lead, expert_count * capacity, 2 * LANES)
    mix_high = mix.astype(jnp.bfloat16)
    mix_low = (mix - mix_high.astype(jnp.float32)).astype(jnp.bfloat16)
    mixed = sum(
        jnp.einsum("nrs,nsc->nrc", part, returned, preferred_element_type=jnp.float32)
        for part in (mix_high, mix_low)
    )
    got = exchange(mixed[:, :, LANES:].astype(jnp.bfloat16), 1)
    mixed = mixed[:, :, :cols] + got[:, :, :cols].astype(jnp.float32)
    return (values + mixed).astype(jnp.bfloat16)


def body(flowing, norm_gain, gate_up, down_proj, down_step, step_rate, routes, scores):
    shards = lax.axis_size("pipe") // step_rate.shape[1]
    my_index = lax.axis_index("pipe")
    section = my_index // shards
    expert_count = lax.axis_size("expert")
    capacity = flowing.shape[1] * routes.shape[-1] // expert_count + 2
    where = jnp.stack([my_index & 3, (my_index >> 3) & 3]).astype(jnp.int32)
    rate = lax.dynamic_slice_in_dim(step_rate[0], section, 1, 0)
    w_in, w_out = arrange_weights(where, rate, gate_up[0, 0], down_proj[0, 0], down_step[0, 0])
    route_here = lax.dynamic_index_in_dim(routes, section, 1, keepdims=False)
    score_here = lax.dynamic_index_in_dim(scores, section, 1, keepdims=False)
    ticks = routes.shape[0]
    state = flowing
    for tick in range(ticks):
        spread, mix = routing(route_here[tick], score_here[tick], expert_count, capacity)
        state = layer(state, spread, mix, norm_gain, w_in, w_out, expert_count, capacity)
        if tick + 1 < ticks:
            state = other_section(state)
    return state


def solution(mesh):
    placed = (
        P(None, "expert", "pipe"),
        P("pipe"),
        P("expert", "pipe", None, None),
        P("expert", "pipe", None, None),
        P("expert", "pipe", None, None),
        P("expert", None),
        P(None, None, None, "expert", None),
        P(None, None, None, "expert", None),
    )
    return jax.shard_map(
        body, mesh=mesh, in_specs=placed, out_specs=P(None, "expert", "pipe"), check_vma=False
    )
```

```python
import jax
import jax.numpy as jnp
from jax import lax
from jax.experimental import pallas as pl
from jax.experimental.pallas import tpu as pltpu
from jax.sharding import PartitionSpec as P

D = 7168
FF = 2048
EPS = 1e-06
ROUTE_SCALE = 2.5
LANES = 256
SQ_TILE = 8
DOT_ROWS = (((1,), (1,)), ((), ()))


def exchange(x, bit):
    size = lax.axis_size("pipe")
    return lax.ppermute(x, "pipe", [(i, i ^ (1 << bit)) for i in range(size)])


def along_y(x, apart):
    size = lax.axis_size("pipe")
    return lax.ppermute(x, "pipe", [(i, i ^ (apart << 3)) for i in range(size)])


def other_section(x):
    size = lax.axis_size("pipe")
    return lax.ppermute(x, "pipe", [(i, (i + size // 2) % size) for i in range(size)])


def weight_kernel(where, gate_up, down, step, rate, w_in, w_out):
    h, y = where[0], where[1]
    cols = gate_up.shape[0] // 4
    w_in[...] = jnp.zeros_like(w_in)
    w_out[...] = jnp.zeros_like(w_out)
    for block in range(4):
        rows = pl.ds(pl.multiple_of((h ^ ((block & 1) * 2 + (block >> 1))) * cols, 32), cols)
        for place, rel in enumerate(range(4)):
            at = pl.multiple_of((y ^ rel) * 128, 128)
            to = slice(block * LANES, block * LANES + cols)
            w_in[to, place * 256 : place * 256 + 128] = gate_up[rows, pl.ds(at, 128)]
            w_in[to, place * 256 + 128 : place * 256 + 256] = gate_up[
                rows, pl.ds(pl.multiple_of(512 + at, 128), 128)
            ]
            w_out[to, place * 128 : place * 128 + 128] = (
                down[rows, pl.ds(at, 128)].astype(jnp.float32)
                + rate[0] * step[rows, pl.ds(at, 128)].astype(jnp.float32)
            ).astype(jnp.bfloat16)


def arrange_weights(where, rate, gate_up, down, step):
    vmem = pl.BlockSpec(memory_space=pltpu.VMEM)
    smem = pl.BlockSpec(memory_space=pltpu.SMEM)
    return pl.pallas_call(
        weight_kernel,
        out_shape=(
            jax.ShapeDtypeStruct((4 * LANES, gate_up.shape[1]), jnp.bfloat16),
            jax.ShapeDtypeStruct((4 * LANES, down.shape[1]), jnp.bfloat16),
        ),
        in_specs=[smem, vmem, vmem, vmem, smem],
        out_specs=(vmem, vmem),
        cost_estimate=pl.CostEstimate(flops=2000000, bytes_accessed=8000000, transcendentals=0),
    )(where, gate_up, down, step, rate)


def routing(route_ids, route_scores, expert_count, capacity):
    lead, rows, picks = route_ids.shape
    flat = route_ids.reshape(lead, rows * picks)
    one_hot = (flat[:, :, None] == jnp.arange(expert_count, dtype=jnp.int32)).astype(jnp.int32)
    position = jnp.sum((jnp.cumsum(one_hot, axis=1) - one_hot) * one_hot, axis=2)
    slot = (flat * capacity + position).reshape(lead, rows, picks)
    slot_ids = jnp.arange(expert_count * capacity, dtype=jnp.int32)
    chosen = (slot[..., None] == slot_ids).astype(jnp.float32)
    mixing = ROUTE_SCALE * route_scores / jnp.sum(route_scores, axis=2, keepdims=True)
    mix = jnp.sum(mixing[..., None] * chosen, axis=2)
    return jnp.sum(chosen, axis=2).astype(jnp.bfloat16), mix


def layer(state, spread, mix, gain, w_in, w_out, expert_count, capacity):
    lead, rows, cols = state.shape
    values = state.astype(jnp.float32)
    squares = jnp.sum(values * values, axis=2, keepdims=True)
    high = squares.astype(jnp.bfloat16)
    low = (squares - high.astype(jnp.float32)).astype(jnp.bfloat16)
    tail = jnp.zeros((lead, rows, LANES - cols - 2), jnp.bfloat16)
    prepared = jnp.concatenate([(values * gain).astype(jnp.bfloat16), high, low, tail], axis=2)
    got, w_in, w_out = lax.optimization_barrier((exchange(prepared, 1), w_in, w_out))
    both = jnp.concatenate([prepared, got], axis=2)
    buffer = jnp.einsum("nrs,nrc->nsc", spread, both, preferred_element_type=jnp.float32)
    buffer = buffer.astype(jnp.bfloat16).reshape(lead, expert_count, capacity, 2 * LANES)
    arrived = lax.all_to_all(
        buffer.transpose(1, 0, 2, 3), "expert", split_axis=0, concat_axis=0, tiled=True
    )
    slots = expert_count * lead * capacity
    arrived = arrived.reshape(slots, 2 * LANES)
    inputs = jnp.concatenate([arrived, exchange(arrived, 0)], axis=1)
    lane = jnp.arange(4 * LANES) % LANES
    marks = ((lane == cols) | (lane == cols + 1)).astype(jnp.bfloat16)
    marks = jnp.broadcast_to(marks[None], (SQ_TILE, 4 * LANES))
    half = slots // 2
    parts = [inputs[:half], inputs[half:]]
    kept = [jnp.dot(part, w_in[:, :256], preferred_element_type=jnp.float32) for part in parts]
    sent = [
        jnp.dot(part, w_in[:, 256:], preferred_element_type=jnp.float32).astype(jnp.bfloat16)
        for part in parts
    ]
    sums = [
        lax.dot_general(marks, part, DOT_ROWS, preferred_element_type=jnp.float32)
        for part in parts
    ]
    sums = [jnp.pad(row, ((0, 0), (0, LANES - half))) for row in sums]
    summed = []
    for partial, blocks, row in zip(kept, sent, sums):
        packed = [
            jnp.concatenate([blocks[:, k * 256 - 256 : k * 256], row.astype(jnp.bfloat16)])
            for k in (3, 2, 1)
        ]
        if summed:
            packed, _ = lax.optimization_barrier((packed, first))
        first = packed
        got = [along_y(message, k) for message, k in zip(packed, (3, 2, 1))]
        got = sum(message.astype(jnp.float32) for message in got)
        summed.append(jnp.concatenate([partial, row]) + got)
    crossed = [total + exchange(total.astype(jnp.bfloat16), 2).astype(jnp.float32) for total in summed]
    hidden = []
    for total in crossed:
        scaling = lax.rsqrt(total[half, :half] / D + EPS)[:, None]
        projected = total[:half] * scaling
        hidden.append(
            (jax.nn.silu(projected[:, :128]) * projected[:, 128:]).astype(jnp.bfloat16)
        )
    outs = []
    for piece in hidden:
        got = [along_y(piece, k) for k in (3, 2, 1)]
        piece = jnp.concatenate([piece, *got[::-1]], axis=1)
        outs.append(
            lax.dot_general(piece, w_out, DOT_ROWS, preferred_element_type=jnp.float32)
        )
    partial = jnp.concatenate(outs)
    got = exchange(partial[:, 2 * LANES :].astype(jnp.bfloat16), 0)
    expert_out = (partial[:, : 2 * LANES] + got.astype(jnp.float32)).astype(jnp.bfloat16)
    expert_out = expert_out.reshape(expert_count, lead, capacity, 2 * LANES)
    returned = lax.all_to_all(expert_out, "expert", split_axis=0, concat_axis=0, tiled=True)
    returned = returned.transpose(1, 0, 2, 3).reshape(lead, expert_count * capacity, 2 * LANES)
    mix_high = mix.astype(jnp.bfloat16)
    mix_low = (mix - mix_high.astype(jnp.float32)).astype(jnp.bfloat16)
    mixed = sum(
        jnp.einsum("nrs,nsc->nrc", part, returned, preferred_element_type=jnp.float32)
        for part in (mix_high, mix_low)
    )
    got = exchange(mixed[:, :, LANES:].astype(jnp.bfloat16), 1)
    mixed = mixed[:, :, :cols] + got[:, :, :cols].astype(jnp.float32)
    return (values + mixed).astype(jnp.bfloat16)


def body(flowing, norm_gain, gate_up, down_proj, down_step, step_rate, routes, scores):
    shards = lax.axis_size("pipe") // step_rate.shape[1]
    my_index = lax.axis_index("pipe")
    section = my_index // shards
    expert_count = lax.axis_size("expert")
    capacity = flowing.shape[1] * routes.shape[-1] // expert_count + 2
    where = jnp.stack([my_index & 3, (my_index >> 3) & 3]).astype(jnp.int32)
    rate = lax.dynamic_slice_in_dim(step_rate[0], section, 1, 0)
    w_in, w_out = arrange_weights(where, rate, gate_up[0, 0], down_proj[0, 0], down_step[0, 0])
    route_here = lax.dynamic_index_in_dim(routes, section, 1, keepdims=False)
    score_here = lax.dynamic_index_in_dim(scores, section, 1, keepdims=False)
    ticks = routes.shape[0]
    state = flowing
    for tick in range(ticks):
        spread, mix = routing(route_here[tick], score_here[tick], expert_count, capacity)
        state = layer(state, spread, mix, norm_gain, w_in, w_out, expert_count, capacity)
        if tick + 1 < ticks:
            state = other_section(state)
    return state


def solution(mesh):
    placed = (
        P(None, "expert", "pipe"),
        P("pipe"),
        P("expert", "pipe", None, None),
        P("expert", "pipe", None, None),
        P("expert", "pipe", None, None),
        P("expert", None),
        P(None, None, None, "expert", None),
        P(None, None, None, "expert", None),
    )
    return jax.shard_map(
        body, mesh=mesh, in_specs=placed, out_specs=P(None, "expert", "pipe"), check_vma=False
    )
```

```python
import jax
import jax.numpy as jnp
from jax import lax
from jax.experimental import pallas as pl
from jax.experimental.pallas import tpu as pltpu
from jax.sharding import PartitionSpec as P

D = 7168
FF = 2048
EPS = 1e-06
ROUTE_SCALE = 2.5
LANES = 256
SQ_TILE = 16
DOT_ROWS = (((1,), (1,)), ((), ()))


def exchange(x, bit):
    size = lax.axis_size("pipe")
    return lax.ppermute(x, "pipe", [(i, i ^ (1 << bit)) for i in range(size)])


def along_y(x, apart):
    size = lax.axis_size("pipe")
    return lax.ppermute(x, "pipe", [(i, i ^ (apart << 3)) for i in range(size)])


def other_section(x):
    size = lax.axis_size("pipe")
    return lax.ppermute(x, "pipe", [(i, (i + size // 2) % size) for i in range(size)])


def weight_kernel(where, gate_up, down, step, rate, w_in, w_out):
    h, y = where[0], where[1]
    cols = gate_up.shape[0] // 4
    w_in[...] = jnp.zeros_like(w_in)
    w_out[...] = jnp.zeros_like(w_out)
    for block in range(4):
        rows = pl.ds(pl.multiple_of((h ^ ((block & 1) * 2 + (block >> 1))) * cols, 32), cols)
        for place, rel in enumerate(range(4)):
            at = pl.multiple_of((y ^ rel) * 128, 128)
            to = slice(block * LANES, block * LANES + cols)
            w_in[to, place * 256 : place * 256 + 128] = gate_up[rows, pl.ds(at, 128)]
            w_in[to, place * 256 + 128 : place * 256 + 256] = gate_up[
                rows, pl.ds(pl.multiple_of(512 + at, 128), 128)
            ]
            w_out[to, place * 128 : place * 128 + 128] = (
                down[rows, pl.ds(at, 128)].astype(jnp.float32)
                + rate[0] * step[rows, pl.ds(at, 128)].astype(jnp.float32)
            ).astype(jnp.bfloat16)


def arrange_weights(where, rate, gate_up, down, step):
    vmem = pl.BlockSpec(memory_space=pltpu.VMEM)
    smem = pl.BlockSpec(memory_space=pltpu.SMEM)
    return pl.pallas_call(
        weight_kernel,
        out_shape=(
            jax.ShapeDtypeStruct((4 * LANES, gate_up.shape[1]), jnp.bfloat16),
            jax.ShapeDtypeStruct((4 * LANES, down.shape[1]), jnp.bfloat16),
        ),
        in_specs=[smem, vmem, vmem, vmem, smem],
        out_specs=(vmem, vmem),
        cost_estimate=pl.CostEstimate(flops=2000000, bytes_accessed=8000000, transcendentals=0),
    )(where, gate_up, down, step, rate)


def routing(route_ids, route_scores, expert_count, capacity):
    lead, rows, picks = route_ids.shape
    flat = route_ids.reshape(lead, rows * picks)
    one_hot = (flat[:, :, None] == jnp.arange(expert_count, dtype=jnp.int32)).astype(jnp.int32)
    position = jnp.sum((jnp.cumsum(one_hot, axis=1) - one_hot) * one_hot, axis=2)
    slot = (flat * capacity + position).reshape(lead, rows, picks)
    slot_ids = jnp.arange(expert_count * capacity, dtype=jnp.int32)
    chosen = (slot[..., None] == slot_ids).astype(jnp.float32)
    mixing = ROUTE_SCALE * route_scores / jnp.sum(route_scores, axis=2, keepdims=True)
    mix = jnp.sum(mixing[..., None] * chosen, axis=2)
    return jnp.sum(chosen, axis=2).astype(jnp.bfloat16), mix


def layer(state, spread, mix, gain, w_in, w_out, expert_count, capacity):
    lead, rows, cols = state.shape
    values = state.astype(jnp.float32)
    squares = jnp.sum(values * values, axis=2, keepdims=True)
    high = squares.astype(jnp.bfloat16)
    low = (squares - high.astype(jnp.float32)).astype(jnp.bfloat16)
    tail = jnp.zeros((lead, rows, LANES - cols - 2), jnp.bfloat16)
    prepared = jnp.concatenate([(values * gain).astype(jnp.bfloat16), high, low, tail], axis=2)
    got, w_in, w_out = lax.optimization_barrier((exchange(prepared, 1), w_in, w_out))
    both = jnp.concatenate([prepared, got], axis=2)
    buffer = jnp.einsum("nrs,nrc->nsc", spread, both, preferred_element_type=jnp.float32)
    buffer = buffer.astype(jnp.bfloat16).reshape(lead, expert_count, capacity, 2 * LANES)
    arrived = lax.all_to_all(
        buffer.transpose(1, 0, 2, 3), "expert", split_axis=0, concat_axis=0, tiled=True
    )
    slots = expert_count * lead * capacity
    arrived = arrived.reshape(slots, 2 * LANES)
    inputs = jnp.concatenate([arrived, exchange(arrived, 0)], axis=1)
    lane = jnp.arange(4 * LANES) % LANES
    marks = ((lane == cols) | (lane == cols + 1)).astype(jnp.bfloat16)
    marks = jnp.broadcast_to(marks[None], (SQ_TILE, 4 * LANES))
    half = LANES
    sums = [
        lax.dot_general(marks, part, DOT_ROWS, preferred_element_type=jnp.float32)
        for part in (inputs[:half], inputs[half:])
    ]
    sums[1] = jnp.pad(sums[1], ((0, 0), (0, 2 * half - slots)))
    index = jnp.arange(SQ_TILE)[:, None]
    sums = jnp.where(index == 0, sums[0], jnp.where(index == 1, sums[1], 0.0))
    partial = jnp.dot(inputs, w_in[:, :256], preferred_element_type=jnp.float32)
    blocks = jnp.dot(inputs, w_in[:, 256:], preferred_element_type=jnp.float32)
    blocks = blocks.astype(jnp.bfloat16)
    got = [
        along_y(
            jnp.concatenate(
                [blocks[:, apart * 256 - 256 : apart * 256], sums.astype(jnp.bfloat16)]
            ),
            apart,
        )
        for apart in (3, 2, 1)
    ]
    got = sum(part.astype(jnp.float32) for part in got)
    partial = partial + got[:slots]
    sums = sums + got[slots:]
    message = jnp.concatenate([partial, sums], axis=0).astype(jnp.bfloat16)
    got = exchange(message, 2).astype(jnp.float32)
    partial = partial + got[:slots]
    sums = sums + got[slots:]
    scaling = lax.rsqrt(jnp.concatenate([sums[0], sums[1, : slots - half]]) / D + EPS)[:, None]
    projected = partial * scaling
    activated = (jax.nn.silu(projected[:, :128]) * projected[:, 128:]).astype(jnp.bfloat16)
    got = [along_y(activated, apart) for apart in (3, 2, 1)]
    activated = jnp.concatenate([activated, *got[::-1]], axis=1)
    partial = lax.dot_general(activated, w_out, DOT_ROWS, preferred_element_type=jnp.float32)
    got = exchange(partial[:, 2 * LANES :].astype(jnp.bfloat16), 0)
    expert_out = (partial[:, : 2 * LANES] + got.astype(jnp.float32)).astype(jnp.bfloat16)
    expert_out = expert_out.reshape(expert_count, lead, capacity, 2 * LANES)
    returned = lax.all_to_all(expert_out, "expert", split_axis=0, concat_axis=0, tiled=True)
    returned = returned.transpose(1, 0, 2, 3).reshape(lead, expert_count * capacity, 2 * LANES)
    mix_high = mix.astype(jnp.bfloat16)
    mix_low = (mix - mix_high.astype(jnp.float32)).astype(jnp.bfloat16)
    mixed = sum(
        jnp.einsum("nrs,nsc->nrc", part, returned, preferred_element_type=jnp.float32)
        for part in (mix_high, mix_low)
    )
    got = exchange(mixed[:, :, LANES:].astype(jnp.bfloat16), 1)
    mixed = mixed[:, :, :cols] + got[:, :, :cols].astype(jnp.float32)
    return (values + mixed).astype(jnp.bfloat16)


def body(flowing, norm_gain, gate_up, down_proj, down_step, step_rate, routes, scores):
    shards = lax.axis_size("pipe") // step_rate.shape[1]
    my_index = lax.axis_index("pipe")
    section = my_index // shards
    expert_count = lax.axis_size("expert")
    capacity = flowing.shape[1] * routes.shape[-1] // expert_count + 2
    where = jnp.stack([my_index & 3, (my_index >> 3) & 3]).astype(jnp.int32)
    rate = lax.dynamic_slice_in_dim(step_rate[0], section, 1, 0)
    w_in, w_out = arrange_weights(where, rate, gate_up[0, 0], down_proj[0, 0], down_step[0, 0])
    route_here = lax.dynamic_index_in_dim(routes, section, 1, keepdims=False)
    score_here = lax.dynamic_index_in_dim(scores, section, 1, keepdims=False)
    ticks = routes.shape[0]
    state = flowing
    for tick in range(ticks):
        spread, mix = routing(route_here[tick], score_here[tick], expert_count, capacity)
        state = layer(state, spread, mix, norm_gain, w_in, w_out, expert_count, capacity)
        if tick + 1 < ticks:
            state = other_section(state)
    return state


def solution(mesh):
    placed = (
        P(None, "expert", "pipe"),
        P("pipe"),
        P("expert", "pipe", None, None),
        P("expert", "pipe", None, None),
        P("expert", "pipe", None, None),
        P("expert", None),
        P(None, None, None, "expert", None),
        P(None, None, None, "expert", None),
    )
    return jax.shard_map(
        body, mesh=mesh, in_specs=placed, out_specs=P(None, "expert", "pipe"), check_vma=False
    )
```
